32 devices in a mesh: qubit: 16 (over z, x, core), head: 2 (over y).
Axes of the slice: x: 2, y: 2, z: 4, core: 2. Of those that a mesh axis runs over, the one named last changes fastest.
Arguments:
- tokens: bfloat16 [128, 256, 512], P('qubit'), may hold values from -6 to 6
- kv_cache: bfloat16 [128, 8, 384, 128], P('qubit', 'head'), may hold values from -6 to 6
- cache_age: int32 [128, 3], P('qubit'), may hold values from 1 to 8
- partner: int32 [128], P('qubit'), may hold values from 0 to 127, as said below
- slope: float32 [8], P('head'), may hold values from 0.03 to 1.5
- w_qkv: bfloat16 [3, 512, 512], P(None, None, 'head'), may hold values from -0.25 to 0.25
- w_o: bfloat16 [512, 512], replicated, may hold values from -0.25 to 0.25
- attn_gain: float32 [512], replicated, may hold values from 0.5 to 1.5
- mlp_gain: float32 [512], replicated, may hold values from 0.5 to 1.5
- w_in: bfloat16 [512, 2048], P(None, 'head'), may hold values from -0.25 to 0.25
- w_down: bfloat16 [2048, 512], P('head'), may hold values from -0.125 to 0.125
Outputs:
- decoded: bfloat16 [128, 256, 512], P('qubit', 'head')
The draws below stay inside these ranges and needn't reach their ends.
Inputs may be any that keep to these rules, and one draw needn't show every extreme that they name: partner pairs the qubits: partner[partner[q]] = q. With H = 8, the 8 qubits of device d (q // 8 = d) carry the colours 0 to 7, one each, in an order drawn per device; the qubit of colour c pairs with the qubit of colour c on device H + (d + c) mod H if d < H, on device (d - H - c) mod H if d >= H.
All inputs are finite; a program needn't handle non-finite values.
Results may differ from the reference program's by a relative error of at most 0.0065.
Values may be sent and summed in bfloat16 or wider, within the bound.
A program may use at most 128 MiB of HBM per device.

```python
import math
import jax
import jax.numpy as jnp
from jax import lax

D = 512
HEADS = 8
DH = 64
FF = 2048
STAB = 128
CACHE_R = 3
Q_DEV = 8
NEW = 256
KEYS = 384
QUBITS = 128


def draw_partner(key, part):
    devices = QUBITS // Q_DEV
    half_count = devices // 2
    second_key = jax.random.fold_in(key, 23)
    colors_row = jnp.arange(Q_DEV, dtype=jnp.int32)
    scores = jax.random.randint(second_key, (devices, Q_DEV), 0, 1 << 20) * Q_DEV + colors_row[None, :]
    order = jnp.argsort(scores, axis=1, stable=True).astype(jnp.int32)
    device_idx = jnp.arange(devices, dtype=jnp.int32)[:, None]
    lower_side = device_idx < half_count
    target_dev = jnp.where(lower_side, half_count + (device_idx + colors_row[None, :]) % half_count, (device_idx - half_count - colors_row[None, :]) % half_count)
    colors = colors_row[None, :]
    source = device_idx * Q_DEV + order
    target = target_dev * Q_DEV + order[target_dev, colors]
    return jnp.zeros((QUBITS,), jnp.int32).at[source.reshape(-1)].set(target.reshape(-1).astype(jnp.int32))


def with_ends(result, own_key, smallest, high):
    place = [jax.random.randint(jax.random.fold_in(own_key, axis), (), 0, length) for axis, length in enumerate(result.shape)]
    main_axis = result.shape.index(max(result.shape))
    beside = place[:main_axis] + [(place[main_axis] + 1) % result.shape[main_axis]] + place[main_axis + 1:]
    return result.at[tuple(place)].set(smallest).at[tuple(beside)].set(high)


def steps_of(own_key, dims, shards, smallest, high):
    level = 1.0
    for position, shards_of in shards:
        draws = jax.random.uniform(jax.random.fold_in(jax.random.fold_in(own_key, 6), position), (shards_of,), jnp.float32, smallest / len(shards), high / len(shards))
        level = level * jnp.repeat(jnp.exp(draws), dims[position] // shards_of).reshape((-1,) + (1,) * (len(dims) - 1 - position))
    return level


def scatter_about(key, shape, scale, most, split=(), held_as=jnp.bfloat16):
    array = scale * jax.random.normal(key, shape, jnp.float32)
    if split:
        array = array * steps_of(key, shape, split, -0.22, 0.18)
    return jnp.clip(array, -most, most).astype(held_as)


def setup_inputs(seed: int = 0) -> dict:
    streams_of = jax.random.split(jax.random.key(seed), 12)
    return {
        "tokens": scatter_about(streams_of[0], (QUBITS, NEW, D), 1.0, 6.0, ((0, 16),)),
        "kv_cache": scatter_about(streams_of[1], (QUBITS, HEADS, KEYS, 2 * DH), 1.0, 6.0, ((0, 16), (1, 2))),
        "cache_age": with_ends(jax.random.randint(streams_of[2], (QUBITS, CACHE_R), 1, 9), jax.random.fold_in(streams_of[2], 1), 1, 8).astype(jnp.int32),
        "partner": draw_partner(jax.random.fold_in(streams_of[11], 71), 0),
        "slope": jnp.clip(jnp.exp(math.log(1.5) - 3.912023 * jax.random.uniform(streams_of[4], (HEADS,), jnp.float32) ** steps_of(streams_of[4], (HEADS,), ((0, 2),), -0.2, 0.2)), 0.03, 1.5),
        "w_qkv": scatter_about(streams_of[5], (3, D, D), D ** -0.5, 0.25, ((2, 2),)),
        "w_o": scatter_about(streams_of[6], (D, D), D ** -0.5, 0.25),
        "attn_gain": jnp.clip(1.0 + 0.1 * jax.random.normal(streams_of[7], (D,), jnp.float32), 0.5, 1.5),
        "mlp_gain": jnp.clip(1.0 + 0.1 * jax.random.normal(streams_of[8], (D,), jnp.float32), 0.5, 1.5),
        "w_in": scatter_about(streams_of[9], (D, FF), D ** -0.5, 0.25, ((1, 2),)),
        "w_down": scatter_about(streams_of[10], (FF, D), FF ** -0.5, 0.125, ((0, 2),)),
    }


def rms_scale(values, gain):
    return values * lax.rsqrt(lax.optimization_barrier(jnp.mean(values * values, axis=-1, keepdims=True)) + 1e-06) * gain

def cache_bias(age_row, slope, new_len):
    key_age = jnp.repeat(age_row.astype(jnp.float32), STAB)
    query_round = (jnp.arange(new_len) // STAB).astype(jnp.float32)
    return -slope[:, None, None] * (key_age[None, None, :] + query_round[None, :, None])

def fresh_bias(slope, new_len):
    round_idx = jnp.arange(new_len) // STAB
    allowed = round_idx[None, :] <= round_idx[:, None]
    distance = (round_idx[:, None] - round_idx[None, :]).astype(jnp.float32)
    return jnp.where(allowed[None], -slope[:, None, None] * distance[None], -1e+30)

def reference(tokens, kv_cache, cache_age, partner, slope, w_qkv, w_o, attn_gain, mlp_gain, w_in, w_down):
    new_len = tokens.shape[1]
    scale = DH ** (-0.5)
    highest = lax.Precision.HIGHEST

    def one_qubit(index):
        widened = tokens[index].astype(jnp.float32)
        normed = rms_scale(widened, attn_gain).astype(jnp.bfloat16)
        queries = jnp.dot(normed, w_qkv[0], preferred_element_type=jnp.float32).astype(jnp.bfloat16).reshape(new_len, HEADS, DH)
        fresh_k = jnp.dot(normed, w_qkv[1], preferred_element_type=jnp.float32).astype(jnp.bfloat16).reshape(new_len, HEADS, DH)
        fresh_v = jnp.dot(normed, w_qkv[2], preferred_element_type=jnp.float32).astype(jnp.bfloat16).reshape(new_len, HEADS, DH)
        mate = partner[index]
        own_cache = kv_cache[index]
        mate_cache = kv_cache[mate]
        key_set = jnp.concatenate([own_cache[..., :DH], mate_cache[..., :DH], jnp.transpose(fresh_k, (1, 0, 2))], axis=1).astype(jnp.float32)
        value_set = jnp.concatenate([own_cache[..., DH:], mate_cache[..., DH:], jnp.transpose(fresh_v, (1, 0, 2))], axis=1).astype(jnp.float32)
        bias = jnp.concatenate([cache_bias(cache_age[index], slope, new_len), cache_bias(cache_age[mate], slope, new_len), fresh_bias(slope, new_len)], axis=2)
        logits = jnp.einsum('thd,hkd->htk', queries.astype(jnp.float32), key_set, precision=highest) * scale + bias
        top = lax.optimization_barrier(jnp.max(logits, axis=-1))
        weights = jnp.exp(logits - top[..., None])
        rounded = weights.astype(jnp.bfloat16).astype(jnp.float32)
        summed = jnp.einsum('htk,hkd->htd', rounded, value_set, precision=highest)
        attended = summed / lax.optimization_barrier(jnp.sum(weights, axis=-1))[..., None]
        attended = jnp.transpose(attended, (1, 0, 2)).reshape(new_len, HEADS * DH).astype(jnp.bfloat16)
        hidden_state = widened + jnp.dot(attended, w_o, preferred_element_type=jnp.float32)
        mlp_in = rms_scale(hidden_state, mlp_gain).astype(jnp.bfloat16)
        activated = jax.nn.gelu(jnp.dot(mlp_in, w_in, preferred_element_type=jnp.float32)).astype(jnp.bfloat16)
        return (hidden_state + jnp.dot(activated, w_down, preferred_element_type=jnp.float32)).astype(jnp.bfloat16)
    return lax.map(one_qubit, jnp.arange(QUBITS, dtype=jnp.int32))
```

```python
import functools

import jax
import jax.numpy as jnp
from jax import lax
from jax.experimental import pallas as pl
from jax.experimental.pallas import tpu as pltpu
from jax.sharding import PartitionSpec as P

DH = 64
STAB = 128
PARTS = 3
F32 = jnp.float32
BF16 = jnp.bfloat16
MESH = pl.DeviceIdType.MESH
VMEM_BYTES = 67043328
ANY_SPEC = pl.BlockSpec(memory_space=pl.ANY)
SMEM_SPEC = pl.BlockSpec(memory_space=pltpu.SMEM)
VMEM_SPEC = pl.BlockSpec(memory_space=pltpu.VMEM)


def mm(a, b):
    return jnp.dot(a, b, preferred_element_type=F32)


def rms(x, gain):
    return x * lax.rsqrt(jnp.mean(x * x, axis=-1, keepdims=True) + 1e-06) * gain


def head_attention(queries, parts):
    tokens = queries.shape[0]
    blocks, tops = [], []
    for keys, _, biases, firsts in parts:
        s = lax.dot_general(keys, queries, (((1,), (1,)), ((), ())), preferred_element_type=F32)
        for i, (bias, first) in enumerate(zip(biases, firsts)):
            block = s[i * STAB : (i + 1) * STAB, first:]
            top = jnp.max(block, axis=0, keepdims=True) + bias
            if first:
                top = jnp.concatenate([jnp.full((1, first), -1e30, F32), top], axis=1)
            blocks.append((block, bias, first))
            tops.append(top)
    top = functools.reduce(jnp.maximum, tops)
    weights, total = [], None
    for block, bias, first in blocks:
        w = jnp.exp(block + (bias - top[:, first:]))
        if first:
            w = jnp.concatenate([jnp.zeros((STAB, first), F32), w], axis=1)
        weights.append(w.astype(BF16))
        total = w if total is None else total + w
    total = jnp.sum(total, axis=0, keepdims=True)
    at, summed = 0, None
    for _, values, biases, _ in parts:
        w = jnp.concatenate(weights[at : at + len(biases)], axis=0)
        at += len(biases)
        term = lax.dot_general(values, w, (((0,), (0,)), ((), ())), preferred_element_type=F32)
        summed = term if summed is None else summed + term
    return summed / total, top + jnp.log(total)


def layer_kernel(
    n_dev,
    partner_ref,
    age_ref,
    slope_ref,
    tokens_hbm,
    cache_hbm,
    w_qkv_hbm,
    w_o_hbm,
    gain1_ref,
    gain2_ref,
    w_in_hbm,
    w_down_hbm,
    out_ref,
    order,
    colour,
    tok,
    cache,
    w_qkv,
    w_o,
    w_in,
    w_dn,
    normed,
    q_send,
    q_recv,
    n_send,
    n_all,
    f_send,
    f_recv,
    result,
    lse_scr,
    load_sem,
    w_ss,
    w_rs,
    q_ss,
    q_rs,
    n_ss,
    n_rs,
    f_ss,
    f_rs,
):
    count, new_len, _ = tok.shape
    heads, keys = cache.shape[1], cache.shape[2]
    hd = heads * DH
    rounds, new_rounds = keys // STAB, new_len // STAB
    rows = out_ref.shape[1]
    half = n_dev // 2
    me = lax.axis_index("qubit").astype(jnp.int32)
    y = lax.axis_index("head").astype(jnp.int32)
    n = n_all.shape[1]

    def beside(r):
        return lax.rem(y + r, n)

    def mate(c):
        return jnp.where(me < half, half + lax.rem(me + c, half), lax.rem(me - c + 2 * half, half))

    def load(i, src, dst):
        return pltpu.make_async_copy(src, dst, load_sem.at[i])

    first_loads = [load(0, tokens_hbm, tok), load(1, w_qkv_hbm, w_qkv)]
    later_loads = [
        load(2, cache_hbm, cache),
        load(3, w_o_hbm, w_o),
        load(4, w_in_hbm, w_in.at[0]),
        load(5, w_down_hbm, w_dn.at[0]),
    ]
    for copy in first_loads:
        copy.start()

    barrier = pltpu.get_barrier_semaphore()
    for c in range(count):
        for t in range(n):
            pl.semaphore_signal(barrier, inc=1, device_id=(mate(c), t), device_id_type=MESH)
    for r in range(1, n):
        pl.semaphore_signal(barrier, inc=1, device_id=(me, beside(r)), device_id_type=MESH)

    tints = []
    for q in range(count):
        owner = lax.div(partner_ref[q], count)
        tints.append(jnp.where(me < half, lax.rem(owner - me + n_dev, half), lax.rem(me - owner + n_dev, half)))
        colour[q] = jnp.minimum(tints[q], count - 1)
    for c in range(count):
        order[c] = functools.reduce(jnp.maximum, [jnp.where(tint == c, q, 0) for q, tint in enumerate(tints)])
    lse_scr[...] = jnp.zeros_like(lse_scr)

    def q_copy(c):
        return pltpu.make_async_remote_copy(
            src_ref=q_send.at[c],
            dst_ref=q_recv.at[c],
            send_sem=q_ss.at[c],
            recv_sem=q_rs.at[c],
            device_id=(mate(c), y),
            device_id_type=MESH,
        )

    def n_copy(c, r):
        return pltpu.make_async_remote_copy(
            src_ref=n_send.at[c, beside(r)],
            dst_ref=n_all.at[c, y],
            send_sem=n_ss.at[c, r],
            recv_sem=n_rs.at[c, y],
            device_id=(me, beside(r)),
            device_id_type=MESH,
        )

    def n_arrival(c, r):
        group = beside(n - r)
        return pltpu.make_async_remote_copy(
            src_ref=n_send.at[c, group],
            dst_ref=n_all.at[c, group],
            send_sem=n_ss.at[c, r],
            recv_sem=n_rs.at[c, group],
            device_id=(me, group),
            device_id_type=MESH,
        )

    def f_copy(c, t):
        return pltpu.make_async_remote_copy(
            src_ref=f_send.at[c, t],
            dst_ref=f_recv.at[c, y],
            send_sem=f_ss.at[c, t],
            recv_sem=f_rs.at[c, y],
            device_id=(mate(c), t),
            device_id_type=MESH,
        )

    def f_arrival(c, group):
        return pltpu.make_async_remote_copy(
            src_ref=f_send.at[c, 0],
            dst_ref=f_recv.at[c, group],
            send_sem=f_ss.at[c, 0],
            recv_sem=f_rs.at[c, group],
            device_id=(mate(c), group),
            device_id_type=MESH,
        )

    def w_copy(i, r, src, dst):
        return pltpu.make_async_remote_copy(
            src_ref=src,
            dst_ref=dst.at[r],
            send_sem=w_ss.at[i, r],
            recv_sem=w_rs.at[i, r],
            device_id=(me, beside(r)),
            device_id_type=MESH,
        )

    w_copies = []
    for r in range(1, n):
        w_copies += [w_copy(0, r, w_in_hbm, w_in), w_copy(1, r, w_down_hbm, w_dn)]

    def project(c):
        x = rms(tok[order[c]].astype(F32), gain1_ref[...]).astype(BF16)
        normed[c] = x
        q_send[c] = (mm(x, w_qkv[0]).astype(BF16) * jnp.asarray(DH**-0.5, BF16)).astype(BF16)

    for copy in first_loads:
        copy.wait()
    project(0)
    for copy in later_loads:
        copy.start()
    project(1)
    pl.semaphore_wait(barrier, n * count + n - 1)

    def send_loop(c, _):
        q_copy(c - 2).start()
        project(c)
        return 0

    lax.fori_loop(2, count, send_loop, 0)
    q_copy(count - 2).start()
    q_copy(count - 1).start()
    for copy in w_copies:
        copy.start()
    later_loads[0].wait()

    def cache_part(row, h):
        kv = cache[row, h]
        biases = [-slope_ref[h] * age_ref[row, r].astype(F32) for r in range(rounds)]
        return kv[:, :DH], kv[:, DH:], biases, [0] * rounds

    def note_lse(h, lse):
        for p in range(PARTS):
            part = lse.astype(BF16).astype(F32)
            lse_scr[p * heads + h : p * heads + h + 1, :] = part
            lse = lse - part

    def put(buffer, c, at, value):
        value = value.astype(BF16)
        for t in range(n):
            buffer[c, t, at, :] = value[:, t * rows : (t + 1) * rows]

    def near(c):
        row = order[c]
        x = normed[c]
        k = mm(x, w_qkv[1]).astype(BF16)
        v = mm(x, w_qkv[2]).astype(BF16)
        for h in range(heads):
            cols = slice(h * DH, (h + 1) * DH)
            slope = slope_ref[h]
            fresh = (
                k[:, cols],
                v[:, cols],
                [slope * float(r) for r in range(new_rounds)],
                [r * STAB for r in range(new_rounds)],
            )
            out, lse = head_attention(q_send[c, :, cols], [cache_part(row, h), fresh])
            put(n_send, c, cols, out)
            note_lse(h, lse)
        put(n_send, c, slice(hd, None), lse_scr[...])
        n_all[c, y] = n_send[c, y]

    def far(c):
        row = order[c]
        for h in range(heads):
            cols = slice(h * DH, (h + 1) * DH)
            out, lse = head_attention(q_recv[c, :, cols], [cache_part(row, h)])
            put(f_send, c, cols, out)
            note_lse(h, lse)
        put(f_send, c, slice(hd, None), lse_scr[...])

    def attend_loop(c, _):
        near(c)
        for r in range(1, n):
            n_copy(c, r).start()
        q_copy(c).wait_recv()
        far(c)
        for t in range(n):
            f_copy(c, t).start()
        return 0

    lax.fori_loop(0, count, attend_loop, 0)

    for copy in later_loads[1:]:
        copy.wait()
    for copy in w_copies:
        copy.wait()

    def lse_of(tile):
        tail = tile[hd:, :].astype(F32)
        return sum(tail[p * heads : (p + 1) * heads] for p in range(PARTS))

    def finish_loop(c, _):
        for r in range(1, n):
            n_arrival(c, r).wait_recv()
        feats = []
        for group in range(n):
            f_arrival(c, group).wait_recv()
            near_part, far_part = n_all[c, group], f_recv[c, group]
            lse_near, lse_far = lse_of(near_part), lse_of(far_part)
            top = jnp.maximum(lse_near, lse_far)
            a, b = jnp.exp(lse_near - top), jnp.exp(lse_far - top)
            a, b = a / (a + b), b / (a + b)
            for h in range(heads):
                cols = slice(h * DH, (h + 1) * DH)
                feats.append(
                    near_part[cols].astype(F32) * a[h : h + 1] + far_part[cols].astype(F32) * b[h : h + 1]
                )
        attended = jnp.transpose(jnp.concatenate(feats, axis=0)).astype(BF16)
        x = tok[order[c], pl.ds(pl.multiple_of(y * rows, rows), rows), :].astype(F32)
        hidden = x + mm(attended, w_o[...])
        mlp_in = rms(hidden, gain2_ref[...]).astype(BF16)
        total = hidden
        for r in range(n):
            total = total + mm(jax.nn.gelu(mm(mlp_in, w_in[r])).astype(BF16), w_dn[r])
        result[c] = total.astype(BF16)
        return 0

    lax.fori_loop(0, count, finish_loop, 0)
    for q in range(count):
        out_ref[q] = result[colour[q]]

    def drain_loop(c, _):
        q_copy(c).wait_send()
        for r in range(1, n):
            n_copy(c, r).wait_send()
        for t in range(n):
            f_copy(c, t).wait_send()
        return 0

    lax.fori_loop(0, count, drain_loop, 0)


def on_device(n_dev, n, tokens, kv_cache, cache_age, partner, slope, w_qkv, w_o, attn_gain, mlp_gain, w_in, w_down):
    count, new_len, width = tokens.shape
    heads = kv_cache.shape[1]
    hd = heads * DH
    rows = new_len // n
    tall = hd + 16
    dma = pltpu.SemaphoreType.DMA
    return pl.pallas_call(
        functools.partial(layer_kernel, n_dev),
        in_specs=[SMEM_SPEC] * 3 + [ANY_SPEC] * 4 + [VMEM_SPEC] * 2 + [ANY_SPEC] * 2,
        out_specs=VMEM_SPEC,
        out_shape=jax.ShapeDtypeStruct((count, rows, width), BF16),
        scratch_shapes=[
            pltpu.SMEM((count,), jnp.int32),
            pltpu.SMEM((count,), jnp.int32),
            pltpu.VMEM(tokens.shape, BF16),
            pltpu.VMEM(kv_cache.shape, BF16),
            pltpu.VMEM(w_qkv.shape, BF16),
            pltpu.VMEM(w_o.shape, BF16),
            pltpu.VMEM((n, *w_in.shape), BF16),
            pltpu.VMEM((n, *w_down.shape), BF16),
            pltpu.VMEM(tokens.shape, BF16),
            pltpu.VMEM((count, new_len, hd), BF16),
            pltpu.VMEM((count, new_len, hd), BF16),
            pltpu.VMEM((count, n, tall, rows), BF16),
            pltpu.VMEM((count, n, tall, rows), BF16),
            pltpu.VMEM((count, n, tall, rows), BF16),
            pltpu.VMEM((count, n, tall, rows), BF16),
            pltpu.VMEM((count, rows, width), BF16),
            pltpu.VMEM((16, new_len), F32),
            dma((6,)),
            dma((2, n)),
            dma((2, n)),
            dma((count,)),
            dma((count,)),
            dma((count, n)),
            dma((count, n)),
            dma((count, n)),
            dma((count, n)),
        ],
        compiler_params=pltpu.CompilerParams(collective_id=0, has_side_effects=True, vmem_limit_bytes=VMEM_BYTES),
        name="layer",
    )(partner, cache_age, slope, tokens, kv_cache, w_qkv, w_o, attn_gain[None], mlp_gain[None], w_in, w_down)


def solution(mesh):
    in_specs = (
        P("qubit", None, None),
        P("qubit", "head", None, None),
        P("qubit", None),
        P("qubit"),
        P("head"),
        P(None, None, "head"),
        P(),
        P(),
        P(),
        P(None, "head"),
        P("head", None),
    )
    return jax.shard_map(
        functools.partial(on_device, mesh.shape["qubit"], mesh.shape["head"]),
        mesh=mesh,
        in_specs=in_specs,
        out_specs=P("qubit", "head", None),
        check_vma=False,
    )
```

```python
import functools

import jax
import jax.numpy as jnp
from jax import lax
from jax.experimental import pallas as pl
from jax.experimental.pallas import tpu as pltpu
from jax.sharding import PartitionSpec as P

DH = 64
STAB = 128
PARTS = 3
F32 = jnp.float32
BF16 = jnp.bfloat16
MESH = pl.DeviceIdType.MESH
VMEM_BYTES = 67043328
ANY_SPEC = pl.BlockSpec(memory_space=pl.ANY)
SMEM_SPEC = pl.BlockSpec(memory_space=pltpu.SMEM)
VMEM_SPEC = pl.BlockSpec(memory_space=pltpu.VMEM)


def mm(a, b):
    return jnp.dot(a, b, preferred_element_type=F32)


def rms(x, gain):
    return x * lax.rsqrt(jnp.mean(x * x, axis=-1, keepdims=True) + 1e-06) * gain


def head_attention(queries, parts):
    tokens = queries.shape[0]
    blocks, tops = [], []
    for keys, _, biases, firsts in parts:
        s = lax.dot_general(keys, queries, (((1,), (1,)), ((), ())), preferred_element_type=F32)
        for i, (bias, first) in enumerate(zip(biases, firsts)):
            block = s[i * STAB : (i + 1) * STAB, first:]
            top = jnp.max(block, axis=0, keepdims=True) + bias
            if first:
                top = jnp.concatenate([jnp.full((1, first), -1e30, F32), top], axis=1)
            blocks.append((block, bias, first))
            tops.append(top)
    top = functools.reduce(jnp.maximum, tops)
    weights, total = [], None
    for block, bias, first in blocks:
        w = jnp.exp(block + (bias - top[:, first:]))
        if first:
            w = jnp.concatenate([jnp.zeros((STAB, first), F32), w], axis=1)
        weights.append(w.astype(BF16))
        total = w if total is None else total + w
    total = jnp.sum(total, axis=0, keepdims=True)
    at, summed = 0, None
    for _, values, biases, _ in parts:
        w = jnp.concatenate(weights[at : at + len(biases)], axis=0)
        at += len(biases)
        term = lax.dot_general(values, w, (((0,), (0,)), ((), ())), preferred_element_type=F32)
        summed = term if summed is None else summed + term
    return summed / total, top + jnp.log(total)


def layer_kernel(
    n_dev,
    partner_ref,
    age_ref,
    slope_ref,
    tokens_hbm,
    cache_hbm,
    w_qkv_hbm,
    w_o_hbm,
    gain1_ref,
    gain2_ref,
    w_in_hbm,
    w_down_hbm,
    out_ref,
    order,
    colour,
    tok,
    cache,
    w_qkv,
    w_o,
    w_in,
    w_dn,
    normed,
    q_send,
    q_recv,
    n_send,
    n_all,
    f_send,
    f_recv,
    l_send,
    l_recv,
    result,
    lse_scr,
    load_sem,
    w_ss,
    w_rs,
    q_ss,
    q_rs,
    n_ss,
    n_rs,
    f_ss,
    f_rs,
    l_ss,
    l_rs,
):
    count, new_len, _ = tok.shape
    heads, keys = cache.shape[1], cache.shape[2]
    hd = heads * DH
    rounds, new_rounds = keys // STAB, new_len // STAB
    rows = out_ref.shape[1]
    half = n_dev // 2
    me = lax.axis_index("qubit").astype(jnp.int32)
    y = lax.axis_index("head").astype(jnp.int32)
    n = n_all.shape[1]

    def beside(r):
        return lax.rem(y + r, n)

    def mate(c):
        return jnp.where(me < half, half + lax.rem(me + c, half), lax.rem(me - c + 2 * half, half))

    def load(i, src, dst):
        return pltpu.make_async_copy(src, dst, load_sem.at[i])

    first_loads = [load(0, tokens_hbm, tok), load(1, w_qkv_hbm, w_qkv)]
    later_loads = [
        load(2, cache_hbm, cache),
        load(3, w_o_hbm, w_o),
        load(4, w_in_hbm, w_in.at[0]),
        load(5, w_down_hbm, w_dn.at[0]),
    ]
    for copy in first_loads:
        copy.start()

    barrier = pltpu.get_barrier_semaphore()
    for c in range(count):
        for t in range(n):
            pl.semaphore_signal(barrier, inc=1, device_id=(mate(c), t), device_id_type=MESH)
    for r in range(1, n):
        pl.semaphore_signal(barrier, inc=1, device_id=(me, beside(r)), device_id_type=MESH)

    tints = []
    for q in range(count):
        owner = lax.div(partner_ref[q], count)
        tints.append(jnp.where(me < half, lax.rem(owner - me + n_dev, half), lax.rem(me - owner + n_dev, half)))
        colour[q] = jnp.minimum(tints[q], count - 1)
    for c in range(count):
        order[c] = functools.reduce(jnp.maximum, [jnp.where(tint == c, q, 0) for q, tint in enumerate(tints)])
    lse_scr[...] = jnp.zeros_like(lse_scr)

    def q_copy(c):
        return pltpu.make_async_remote_copy(
            src_ref=q_send.at[c],
            dst_ref=q_recv.at[c],
            send_sem=q_ss.at[c],
            recv_sem=q_rs.at[c],
            device_id=(mate(c), y),
            device_id_type=MESH,
        )

    def n_copy(c, r):
        return pltpu.make_async_remote_copy(
            src_ref=n_send.at[c, beside(r)],
            dst_ref=n_all.at[c, y],
            send_sem=n_ss.at[c, r],
            recv_sem=n_rs.at[c, y],
            device_id=(me, beside(r)),
            device_id_type=MESH,
        )

    def n_arrival(c, r):
        group = beside(n - r)
        return pltpu.make_async_remote_copy(
            src_ref=n_send.at[c, group],
            dst_ref=n_all.at[c, group],
            send_sem=n_ss.at[c, r],
            recv_sem=n_rs.at[c, group],
            device_id=(me, group),
            device_id_type=MESH,
        )

    far_pairs = ((f_send, f_recv, f_ss, f_rs), (l_send, l_recv, l_ss, l_rs))

    def f_copies(c, t):
        return [
            pltpu.make_async_remote_copy(
                src_ref=src.at[c, t],
                dst_ref=dst.at[c, y],
                send_sem=ss.at[c, t],
                recv_sem=rs.at[c, y],
                device_id=(mate(c), t),
                device_id_type=MESH,
            )
            for src, dst, ss, rs in far_pairs
        ]

    def f_arrivals(c, group):
        return [
            pltpu.make_async_remote_copy(
                src_ref=src.at[c, 0],
                dst_ref=dst.at[c, group],
                send_sem=ss.at[c, 0],
                recv_sem=rs.at[c, group],
                device_id=(mate(c), group),
                device_id_type=MESH,
            )
            for src, dst, ss, rs in far_pairs
        ]

    def w_copy(i, r, src, dst):
        return pltpu.make_async_remote_copy(
            src_ref=src,
            dst_ref=dst.at[r],
            send_sem=w_ss.at[i, r],
            recv_sem=w_rs.at[i, r],
            device_id=(me, beside(r)),
            device_id_type=MESH,
        )

    w_copies = []
    for r in range(1, n):
        w_copies += [w_copy(0, r, w_in_hbm, w_in), w_copy(1, r, w_down_hbm, w_dn)]

    def project(c):
        x = rms(tok[order[c]].astype(F32), gain1_ref[...]).astype(BF16)
        normed[c] = x
        q_send[c] = (mm(x, w_qkv[0]).astype(BF16) * jnp.asarray(DH**-0.5, BF16)).astype(BF16)

    for copy in first_loads:
        copy.wait()
    project(0)
    for copy in later_loads:
        copy.start()
    project(1)
    pl.semaphore_wait(barrier, n * count + n - 1)

    def send_loop(c, _):
        q_copy(c - 2).start()
        project(c)
        return 0

    lax.fori_loop(2, count, send_loop, 0)
    q_copy(count - 2).start()
    q_copy(count - 1).start()
    for copy in w_copies:
        copy.start()
    later_loads[0].wait()

    def cache_part(row, h):
        kv = cache[row, h]
        biases = [-slope_ref[h] * age_ref[r, row].astype(F32) for r in range(rounds)]
        return kv[:, :DH], kv[:, DH:], biases, [0] * rounds

    def note_lse(h, lse):
        for p in range(PARTS):
            part = lse.astype(BF16).astype(F32)
            lse_scr[p * heads + h : p * heads + h + 1, :] = part
            lse = lse - part

    def put(buffer, c, at, value):
        value = value.astype(BF16)
        for t in range(n):
            buffer[c, t, at, :] = value[:, t * rows : (t + 1) * rows]

    def near(c):
        row = order[c]
        x = normed[c]
        k = mm(x, w_qkv[1]).astype(BF16)
        v = mm(x, w_qkv[2]).astype(BF16)
        for h in range(heads):
            cols = slice(h * DH, (h + 1) * DH)
            slope = slope_ref[h]
            fresh = (
                k[:, cols],
                v[:, cols],
                [slope * float(r) for r in range(new_rounds)],
                [r * STAB for r in range(new_rounds)],
            )
            out, lse = head_attention(q_send[c, :, cols], [cache_part(row, h), fresh])
            put(n_send, c, cols, out)
            note_lse(h, lse)
        put(n_send, c, slice(hd, None), lse_scr[...])
        n_all[c, y] = n_send[c, y]

    def far(c):
        row = order[c]
        for h in range(heads):
            cols = slice(h * DH, (h + 1) * DH)
            out, lse = head_attention(q_recv[c, :, cols], [cache_part(row, h)])
            put(f_send, c, cols, out)
            for t in range(n):
                l_send[c, t, h : h + 1, :] = lse[:, t * rows : (t + 1) * rows]

    def attend_loop(c, _):
        near(c)
        for r in range(1, n):
            n_copy(c, r).start()
        q_copy(c).wait_recv()
        far(c)
        for t in range(n):
            for copy in f_copies(c, t):
                copy.start()
        return 0

    lax.fori_loop(0, count, attend_loop, 0)

    for copy in later_loads[1:]:
        copy.wait()
    for copy in w_copies:
        copy.wait()

    def lse_of(tile):
        tail = tile[hd:, :].astype(F32)
        return sum(tail[p * heads : (p + 1) * heads] for p in range(PARTS))

    def finish_loop(c, _):
        for r in range(1, n):
            n_arrival(c, r).wait_recv()
        feats = []
        for group in range(n):
            for copy in f_arrivals(c, group):
                copy.wait_recv()
            near_part, far_part = n_all[c, group], f_recv[c, group]
            lse_near, lse_far = lse_of(near_part), l_recv[c, group]
            top = jnp.maximum(lse_near, lse_far)
            a, b = jnp.exp(lse_near - top), jnp.exp(lse_far - top)
            a, b = a / (a + b), b / (a + b)
            for h in range(heads):
                cols = slice(h * DH, (h + 1) * DH)
                feats.append(
                    near_part[cols].astype(F32) * a[h : h + 1] + far_part[cols].astype(F32) * b[h : h + 1]
                )
        attended = jnp.transpose(jnp.concatenate(feats, axis=0)).astype(BF16)
        x = tok[order[c], pl.ds(pl.multiple_of(y * rows, rows), rows), :].astype(F32)
        hidden = x + mm(attended, w_o[...])
        mlp_in = rms(hidden, gain2_ref[...]).astype(BF16)
        total = hidden
        for r in range(n):
            total = total + mm(jax.nn.gelu(mm(mlp_in, w_in[r])).astype(BF16), w_dn[r])
        result[c] = total.astype(BF16)
        return 0

    lax.fori_loop(0, count, finish_loop, 0)
    for q in range(count):
        out_ref[q] = result[colour[q]]

    def drain_loop(c, _):
        q_copy(c).wait_send()
        for r in range(1, n):
            n_copy(c, r).wait_send()
        for t in range(n):
            for copy in f_copies(c, t):
                copy.wait_send()
        return 0

    lax.fori_loop(0, count, drain_loop, 0)


def on_device(n_dev, n, tokens, kv_cache, cache_age, partner, slope, w_qkv, w_o, attn_gain, mlp_gain, w_in, w_down):
    count, new_len, width = tokens.shape
    heads = kv_cache.shape[1]
    hd = heads * DH
    rows = new_len // n
    tall = hd + 16
    dma = pltpu.SemaphoreType.DMA
    return pl.pallas_call(
        functools.partial(layer_kernel, n_dev),
        in_specs=[SMEM_SPEC] * 3 + [ANY_SPEC] * 4 + [VMEM_SPEC] * 2 + [ANY_SPEC] * 2,
        out_specs=VMEM_SPEC,
        out_shape=jax.ShapeDtypeStruct((count, rows, width), BF16),
        scratch_shapes=[
            pltpu.SMEM((count,), jnp.int32),
            pltpu.SMEM((count,), jnp.int32),
            pltpu.VMEM(tokens.shape, BF16),
            pltpu.VMEM(kv_cache.shape, BF16),
            pltpu.VMEM(w_qkv.shape, BF16),
            pltpu.VMEM(w_o.shape, BF16),
            pltpu.VMEM((n, *w_in.shape), BF16),
            pltpu.VMEM((n, *w_down.shape), BF16),
            pltpu.VMEM(tokens.shape, BF16),
            pltpu.VMEM((count, new_len, hd), BF16),
            pltpu.VMEM((count, new_len, hd), BF16),
            pltpu.VMEM((count, n, tall, rows), BF16),
            pltpu.VMEM((count, n, tall, rows), BF16),
            pltpu.VMEM((count, n, hd, rows), BF16),
            pltpu.VMEM((count, n, hd, rows), BF16),
            pltpu.VMEM((count, n, heads, rows), F32),
            pltpu.VMEM((count, n, heads, rows), F32),
            pltpu.VMEM((count, rows, width), BF16),
            pltpu.VMEM((16, new_len), F32),
            dma((6,)),
            dma((2, n)),
            dma((2, n)),
            dma((count,)),
            dma((count,)),
            dma((count, n)),
            dma((count, n)),
            dma((count, n)),
            dma((count, n)),
            dma((count, n)),
            dma((count, n)),
        ],
        compiler_params=pltpu.CompilerParams(collective_id=0, has_side_effects=True, vmem_limit_bytes=VMEM_BYTES),
        name="layer",
    )(partner, cache_age.T, slope, tokens, kv_cache, w_qkv, w_o, attn_gain[None], mlp_gain[None], w_in, w_down)


def solution(mesh):
    in_specs = (
        P("qubit", None, None),
        P("qubit", "head", None, None),
        P("qubit", None),
        P("qubit"),
        P("head"),
        P(None, None, "head"),
        P(),
        P(),
        P(),
        P(None, "head"),
        P("head", None),
    )
    return jax.shard_map(
        functools.partial(on_device, mesh.shape["qubit"], mesh.shape["head"]),
        mesh=mesh,
        in_specs=in_specs,
        out_specs=P("qubit", "head", None),
        check_vma=False,
    )
```
